32 devices in a mesh: grp: 4 (over x, core), wf: 8 (over z, y).
Axes of the slice: x: 2, y: 2, z: 4, core: 2. Of those that a mesh axis runs over, the one named last changes fastest.
Arguments:
- quasi: float32 [32, 4, 262144], P(('grp', 'wf')), may hold values from -6 to 6
- outer_field: float32 [262144], replicated, may hold values from -4 to 4
- coupling: float32 [262144], replicated, may hold values from 2 to 16
Outputs:
- evolved: float32 [32, 4, 262144], P(('grp', 'wf'))
- potentials: float32 [3, 64, 4096], P(None, 'grp', 'wf')
The draws below stay inside these ranges and needn't reach their ends.
All inputs are finite; a program needn't handle non-finite values.
Results may differ from the reference program's by a relative error of at most 0.0003.
Values sent between devices are 32-bit elements; how exact they have to be, the bound alone decides.
No kernel may reach another device: no remote copies, remote signals or barrier semaphores. Data moves between devices by JAX's collectives and lax.ppermute only.
A program may use at most 192 MiB of HBM per device.

```python
import math
import jax
import jax.numpy as jnp
from jax import lax

NX = 64
NG = 64
WAVES = 32
CELLS = 262144


def levels(own_key, shape, cuts, low, high):
    gain, own = 1.0, jax.random.fold_in(own_key, 6)
    for axis_at, blocks in cuts:
        steps = jnp.exp(jax.random.uniform(jax.random.fold_in(own, axis_at), (blocks,), jnp.float32, low / len(cuts), high / len(cuts)))
        gain = gain * jnp.repeat(steps, shape[axis_at] // blocks).reshape([-1 if axis == axis_at else 1 for axis in range(len(shape))])
    return gain


def bell_draw(key, shape, deviation, bound, shards=(), kind=jnp.bfloat16):
    drawn = deviation * jax.random.normal(key, shape, jnp.float32)
    if shards:
        drawn = drawn * levels(key, shape, shards, -0.22, 0.18)
    return jnp.clip(drawn, -bound, bound).astype(kind)


def setup_inputs(seed: int = 0) -> dict:
    keys = jax.random.split(jax.random.key(seed), 4)
    quasi = bell_draw(keys[0], (WAVES, 4, CELLS), 1.0, 6.0, ((0, 32),), jnp.float32)
    outer_field = bell_draw(keys[1], (CELLS,), 1.0, 4.0, (), jnp.float32)
    coupling = jnp.clip(jnp.exp(jax.random.uniform(keys[2], (CELLS,), jnp.float32, math.log(2.0), math.log(16.0))), 2.0, 16.0)
    return {"quasi": quasi, "outer_field": outer_field, "coupling": coupling}


time_step = 0.2
kinetic_coef = 0.5
density_coef = 1.0
coulomb_coef = 0.25


def neighbour_sum(field, first, grid):
    positions = jnp.arange(first * grid * grid, dtype=jnp.int32)
    depth_index = positions % grid
    column_index = (positions // grid) % grid
    plane = grid * grid
    total = jnp.roll(field, plane, -1) + jnp.roll(field, -plane, -1)
    total = total + jnp.where(column_index == grid - 1, jnp.roll(field, (grid - 1) * grid, -1), jnp.roll(field, -grid, -1))
    total = total + jnp.where(column_index == 0, jnp.roll(field, -(grid - 1) * grid, -1), jnp.roll(field, grid, -1))
    total = total + jnp.where(depth_index == grid - 1, jnp.roll(field, grid - 1, -1), jnp.roll(field, -1, -1))
    total = total + jnp.where(depth_index == 0, jnp.roll(field, 1 - grid, -1), jnp.roll(field, 1, -1))
    return total - 6.0 * field


def hamiltonian(state, laplace, fields):
    mean_field, pair_real, pair_imag = fields[0], fields[1], fields[2]
    single = -kinetic_coef * laplace + mean_field * state
    first = single[..., 0, :] + pair_real * state[..., 2, :] - pair_imag * state[..., 3, :]
    second = single[..., 1, :] + pair_real * state[..., 3, :] + pair_imag * state[..., 2, :]
    third = pair_real * state[..., 0, :] + pair_imag * state[..., 1, :] - single[..., 2, :]
    fourth = pair_real * state[..., 1, :] - pair_imag * state[..., 0, :] - single[..., 3, :]
    return jnp.stack([first, second, third, fourth], axis=-2)


def propagate(state, laplace, fields, first, grid):
    result = state
    term = state
    for degree in range(1, 5):
        current = laplace if degree == 1 else neighbour_sum(term, first, grid)
        applied = hamiltonian(term, current, fields)
        factor = time_step / degree
        term = jnp.stack([factor * applied[..., 1, :], -factor * applied[..., 0, :],
                          factor * applied[..., 3, :], -factor * applied[..., 2, :]], axis=-2)
        result = result + term
    return result


def lattice_symbol(indices, length):
    return 2.0 - 2.0 * jnp.cos((2.0 * math.pi / length) * indices.astype(jnp.float32))


def reference(quasi, outer_field, coupling):
    def accumulate(carry, state):
        parts = jnp.stack([state[2] * state[2] + state[3] * state[3],
                           state[0] * state[2] + state[1] * state[3],
                           state[1] * state[2] - state[0] * state[3]])
        return carry + parts, None

    summed, unused = lax.scan(accumulate, jnp.zeros((3, CELLS), jnp.float32), quasi)
    summed = summed / WAVES
    symbol_first = lattice_symbol(jnp.arange(NX, dtype=jnp.int32), NX)
    symbol = lattice_symbol(jnp.arange(NG, dtype=jnp.int32), NG)
    squared = symbol_first[:, None, None] + symbol[None, :, None] + symbol[None, None, :]
    kernel = jnp.where(squared > 1e-3, 4.0 * math.pi * coulomb_coef / jnp.where(squared > 1e-3, squared, 1.0), 0.0)
    spectrum = jnp.fft.fftn(summed[0].reshape(NX, NG, NG))
    coulomb = jnp.real(jnp.fft.ifftn(spectrum * kernel)).astype(jnp.float32).reshape(-1)
    fields = jnp.stack([outer_field + density_coef * summed[0] + coulomb,
                        -coupling * summed[1], -coupling * summed[2]])

    def evolve_one(state):
        return propagate(state, neighbour_sum(state, NX, NG), fields, NX, NG)

    evolved = lax.map(evolve_one, quasi)
    return evolved, fields.reshape(3, NX, NG * NG)
```

```python
import functools
import math

import jax
import jax.numpy as jnp
import numpy as np
from jax import lax
from jax.experimental import pallas as pl
from jax.experimental.pallas import tpu as pltpu
from jax.sharding import PartitionSpec as P

NX = 64
NG = 64
LANES = 2 * NG
PLANE = NG * NG // LANES
ROWS = NX * PLANE
AXES = ("grp", "wf")
GROUP = 4
PAD = 8
PADDED = PLANE + 2 * PAD

time_step = 0.2
kinetic_coef = 0.5
density_coef = 1.0
coulomb_coef = 0.25

F32 = jnp.float32
BF16 = jnp.bfloat16


def fourier_basis(length):
    cells = np.arange(length)
    rows, waves = [np.ones(length) / math.sqrt(length)], [0]
    for wave in range(1, length // 2):
        angle = 2.0 * math.pi * (wave * cells % length) / length
        rows += [math.sqrt(2.0 / length) * np.cos(angle), math.sqrt(2.0 / length) * np.sin(angle)]
        waves += [wave, wave]
    rows.append(np.where(cells % 2 == 0, 1.0, -1.0) / math.sqrt(length))
    waves.append(length // 2)
    return np.stack(rows), np.array(waves)


def lattice_symbol(waves, length):
    return 2.0 - 2.0 * np.cos(2.0 * math.pi / length * waves)


def split(matrix):
    high = matrix.astype(np.float32).astype(jnp.bfloat16)
    low = (matrix - high.astype(np.float64)).astype(jnp.bfloat16)
    return np.stack([high, low])


def block_diagonal(matrix, count):
    return np.kron(np.eye(count), matrix)


def transform_tables():
    basis, waves = fourier_basis(NG)
    order = np.concatenate([np.arange(0, NG, 2), np.arange(1, NG, 2)])
    forward_y = block_diagonal(basis[:, order], GROUP)
    forward_z = block_diagonal(basis.T, 2)
    first, first_waves = fourier_basis(NX)
    even, odd = first_waves % 2 == 0, first_waves % 2 == 1
    symbol_x = lattice_symbol(first_waves, NX)
    symbol = lattice_symbol(waves, NG)
    symbol_xz = np.concatenate(
        [symbol_x[even][:, None] + symbol[None], symbol_x[odd][:, None] + symbol[None]], axis=1
    )
    return dict(
        forward_y=split(forward_y),
        forward_z=split(forward_z),
        inverse_y=split(forward_y.T),
        inverse_z=split(forward_z.T),
        even=first[even][:, : NX // 2].astype(np.float32),
        odd=first[odd][:, : NX // 2].astype(np.float32),
        symbol_xz=symbol_xz.astype(np.float32),
        symbol_y=symbol.astype(np.float32),
    )


class Plan:
    def __init__(self, sizes, orders, pieces):
        self.sizes = sizes
        self.orders = orders
        self.pieces = pieces
        self.halvings = int(math.log2(pieces)) - 1
        kept = [("grp", 1)] + sorted(orders[0][: self.halvings])
        assert kept[1:] == sorted(orders[1][: self.halvings])
        self.kept = kept

    def permutation(self, step):
        pairs = []
        for grp in range(self.sizes["grp"]):
            for wf in range(self.sizes["wf"]):
                axis, mask = ("grp", 1) if step < 0 else self.orders[grp & 1][step]
                to = (grp ^ mask, wf) if axis == "grp" else (grp, wf ^ mask)
                pairs.append((grp * self.sizes["wf"] + wf, to[0] * self.sizes["wf"] + to[1]))
        return pairs

    def identity(self, grp, wf):
        number = 0
        for place, (axis, mask) in enumerate(self.kept):
            value = grp if axis == "grp" else wf
            number = number + (((value >> int(math.log2(mask))) & 1) << place)
        return number

    def piece(self, index, side):
        grp, wf = lax.axis_index("grp"), lax.axis_index("wf")
        core = (grp & 1) ^ side
        grp = grp ^ side
        for step in range(self.halvings):
            bit = (index >> (self.halvings - 1 - step)) & 1
            masks = [
                [mask if axis == name else 0 for axis, mask in (self.orders[0][step], self.orders[1][step])]
                for name in AXES
            ]
            grp_mask = masks[0][0] + core * (masks[0][1] - masks[0][0])
            wf_mask = masks[1][0] + core * (masks[1][1] - masks[1][0])
            grp = grp ^ (bit * grp_mask)
            wf = wf ^ (bit * wf_mask)
        return self.identity(grp, wf)


def reduce_scatter(plan, own, other):
    for step in range(-1, len(plan.orders[0])):
        received = lax.ppermute(other, AXES, plan.permutation(step))
        if step + 1 == len(plan.orders[0]):
            break
        if step + 1 < plan.halvings:
            half = own.shape[0] // 2
            own, other = own[:half] + received[:half], own[half:] + received[half:]
        else:
            own = own + received
            other = own
    return own, received


def all_gather(plan, piece):
    parts = [piece]
    for step in reversed(range(plan.halvings)):
        whole = parts[0] if len(parts) == 1 else jnp.concatenate(parts)
        parts = [whole, lax.ppermute(whole, AXES, plan.permutation(step))]
    return parts + [lax.ppermute(part, AXES, plan.permutation(-1)) for part in parts]


def lane(shape):
    return lax.broadcasted_iota(jnp.int32, shape, len(shape) - 1)


def swap(value):
    return pltpu.roll(value, NG, value.ndim - 1)


def cut(value):
    high = value.astype(BF16)
    return high, (value - high.astype(F32)).astype(BF16)


def product(left, right):
    return lax.dot_general(left, right, (((1,), (0,)), ((), ())), preferred_element_type=F32)


def times_table(value, table):
    high, low = cut(value)
    return product(high, table[0]) + (product(low, table[0]) + product(high, table[1]))


def table_times(table, value):
    high, low = cut(value)
    return product(table[0], high) + (product(table[0], low) + product(table[1], high))


def component(state_ref, wave, index, row, rows):
    return state_ref[pl.ds((wave * ROWS + row) * 4 + index, rows, stride=4), :]


def kappa_kernel(plans, waves, scale, state_ref, *out_refs):
    for which, plan in enumerate(plans):
        rows = ROWS // plan.pieces
        for side in range(2):
            out_ref = out_refs[2 * which + side]

            def body(index, carry, plan=plan, side=side, out_ref=out_ref, which=which, rows=rows):
                row = plan.piece(index, side) * rows
                total = None
                for wave in range(waves):
                    u_real, u_imag, v_real, v_imag = (
                        component(state_ref, wave, c, row, rows) for c in range(4)
                    )
                    if which == 0:
                        value = u_real * v_real + u_imag * v_imag
                    else:
                        value = u_imag * v_real - u_real * v_imag
                    total = value if total is None else total + value
                out_ref[index] = total * scale
                return carry

            lax.fori_loop(0, plan.pieces // 2, body, 0)


def density_kernel(plan, waves, scale, state_ref, y_ref, z_ref, own_ref, other_ref, spectrum_ref):
    low_lanes = lane((PLANE, LANES)) < NG
    half = NX // 2

    def density(plane):
        total = None
        for wave in range(waves):
            real = component(state_ref, wave, 2, plane * PLANE, PLANE)
            imag = component(state_ref, wave, 3, plane * PLANE, PLANE)
            value = real * real + imag * imag
            total = value if total is None else total + value
        return total * scale

    def body(group, carry):
        parts = []
        for j in range(GROUP):
            plane = group * GROUP + j
            first, second = density(plane), density(plane + half)
            parts.append(jnp.where(low_lanes, first, swap(second)))
            parts.append(jnp.where(low_lanes, swap(first), second))
        value = times_table(jnp.concatenate(parts), z_ref)
        value = table_times(y_ref, value)
        for j in range(GROUP):
            spectrum_ref[pl.ds(group * GROUP + j, NG, stride=half), :] = value[j * NG : (j + 1) * NG]
        return carry

    lax.fori_loop(0, half // GROUP, body, 0)
    rows = ROWS // plan.pieces
    for side, out_ref in enumerate((own_ref, other_ref)):

        def place(index, carry, side=side, out_ref=out_ref):
            start = pl.multiple_of(plan.piece(index, side) * rows, 8)
            out_ref[index] = spectrum_ref[pl.ds(start, rows), :]
            return carry

        lax.fori_loop(0, plan.pieces // 2, place, 0)


def coulomb_kernel(plan, own_ref, received_ref, even_ref, odd_ref, xz_ref, y_ref, out_ref):
    half = NX // 2
    low_lanes = lane((half, LANES)) < NG
    sign = jnp.where(low_lanes, 1.0, -1.0)
    count = ROWS // plan.pieces // half
    first = plan.identity(lax.axis_index("grp"), lax.axis_index("wf")) * count

    def dot(matrix, value, axis):
        return lax.dot_general(
            matrix, value, (((axis,), (0,)), ((), ())),
            precision=lax.Precision.HIGHEST, preferred_element_type=F32,
        )

    for k in range(count):
        rows = pl.ds(k * half, half)
        value = own_ref[0, rows, :] + received_ref[0, rows, :]
        value = swap(value) + sign * value
        value = jnp.where(low_lanes, dot(even_ref[...], value, 1), dot(odd_ref[...], value, 1))
        squared = xz_ref[...] + y_ref[first + k]
        kernel = jnp.where(
            squared > 0.001,
            4.0 * math.pi * coulomb_coef / jnp.where(squared > 0.001, squared, 1.0),
            0.0,
        )
        value = value * (density_coef + kernel)
        value = jnp.where(low_lanes, dot(even_ref[...], value, 0), dot(odd_ref[...], value, 0))
        out_ref[0, rows, :] = swap(value) + sign * value


def spread(plan, part_refs, store):
    count = plan.pieces // 4
    for side in range(2):
        for part in range(2):
            ref = part_refs[2 * side + part]

            def body(index, carry, side=side, part=part, ref=ref):
                store(plan.piece(index + part * count, side), ref[index])
                return carry

            lax.fori_loop(0, count, body, 0)


def mean_kernel(plan, *refs):
    part_refs, (outer_ref, y_ref, z_ref, out_ref, spectrum_ref) = refs[:4], refs[4:]
    rows = ROWS // plan.pieces
    half = NX // 2
    low_lanes = lane((PLANE, LANES)) < NG

    def store(piece, value):
        spectrum_ref[pl.ds(pl.multiple_of(piece * rows, 8), rows), :] = value

    spread(plan, part_refs, store)

    def body(group, carry):
        value = jnp.concatenate(
            [spectrum_ref[pl.ds(group * GROUP + j, NG, stride=half), :] for j in range(GROUP)]
        )
        value = table_times(y_ref, value)
        value = times_table(value, z_ref)
        for j in range(GROUP):
            plane = group * GROUP + j
            even = value[j * NG : j * NG + PLANE]
            odd = value[j * NG + PLANE : (j + 1) * NG]
            near = pl.ds(pl.multiple_of(plane * PLANE, 8), PLANE)
            far = pl.ds(pl.multiple_of((plane + half) * PLANE, 8), PLANE)
            out_ref[near, :] = jnp.where(low_lanes, even, swap(odd)) + outer_ref[near, :]
            out_ref[far, :] = jnp.where(low_lanes, swap(even), odd) + outer_ref[far, :]
        return carry

    lax.fori_loop(0, half // GROUP, body, 0)


def propagate_kernel(plans, *refs):
    (state_ref, mean_ref, coupling_ref), refs = refs[:3], refs[3:]
    parts, refs = (refs[:4], refs[4:8]), refs[8:]
    out_ref, potentials_ref, shifted_ref, pair_real_ref, pair_imag_ref, psi_ref, ping_ref, pong_ref = refs
    pairs = (pair_real_ref, pair_imag_ref)

    for plan, part_refs, pair_ref in zip(plans, parts, pairs):
        rows = ROWS // plan.pieces

        def store(piece, value, pair_ref=pair_ref, rows=rows):
            where = pl.ds(pl.multiple_of(piece * rows, 8), rows)
            pair_ref[where, :] = -coupling_ref[where, :] * value

        spread(plan, part_refs, store)

    planes, width = potentials_ref.shape[1:]
    start = lax.axis_index("grp") * planes * PLANE + lax.axis_index("wf") * (width // LANES)
    for which, ref in enumerate((mean_ref, pair_real_ref, pair_imag_ref)):
        for j in range(width // LANES):
            potentials_ref[which, :, j * LANES : (j + 1) * LANES] = ref[pl.ds(start + j, planes, stride=PLANE), :]

    def write(ref, c, plane, chunk, value):
        base = pl.multiple_of(plane * PADDED, 8)
        ref[c, pl.ds(base + PAD + chunk * 8, 8), :] = value
        if chunk == 0:
            ref[c, pl.ds(base + PAD + PLANE, 1), :] = value[:1]
        if chunk == PLANE // 8 - 1:
            ref[c, pl.ds(base + PAD - 1, 1), :] = value[7:]

    def prepare(plane, carry):
        for chunk in range(PLANE // 8):
            row = plane * PLANE + chunk * 8
            where = pl.ds(pl.multiple_of(row, 8), 8)
            shifted_ref[where, :] = mean_ref[where, :] + 6.0 * kinetic_coef
            for c in range(4):
                write(psi_ref, c, plane, chunk, component(state_ref, 0, c, row, 8))
        return carry

    lax.fori_loop(0, NX, prepare, 0)

    lanes = lane((8, LANES))
    high_lanes = lanes >= NG
    last_depth = lanes % NG == NG - 1
    first_depth = lanes % NG == 0

    def stage(degree, source, target):
        factor = time_step / degree

        def body(plane, carry):
            base = pl.multiple_of(plane * PADDED, 8)
            before = pl.multiple_of((plane + NX - 1) % NX * PADDED, 8)
            after = pl.multiple_of((plane + 1) % NX * PADDED, 8)
            for chunk in range(PLANE // 8):
                offset = PAD + chunk * 8
                row = plane * PLANE + chunk * 8
                where = pl.ds(pl.multiple_of(row, 8), 8)
                shifted, pair_real, pair_imag = shifted_ref[where, :], pair_real_ref[where, :], pair_imag_ref[where, :]
                state, single = [], []
                for c in range(4):
                    here = source[c, pl.ds(base + offset, 8), :]
                    total = source[c, pl.ds(before + offset, 8), :] + source[c, pl.ds(after + offset, 8), :]
                    other = swap(here)
                    side = jnp.where(
                        high_lanes,
                        source[c, pl.ds(base + offset - 1, 8), :],
                        source[c, pl.ds(base + offset + 1, 8), :],
                    )
                    total = total + other + swap(side)
                    total = total + pltpu.roll(jnp.where(last_depth, other, here), 1, 1)
                    total = total + pltpu.roll(jnp.where(first_depth, other, here), LANES - 1, 1)
                    state.append(here)
                    single.append(shifted * here - kinetic_coef * total)
                applied = (
                    single[0] + pair_real * state[2] - pair_imag * state[3],
                    single[1] + pair_real * state[3] + pair_imag * state[2],
                    pair_real * state[0] + pair_imag * state[1] - single[2],
                    pair_real * state[1] - pair_imag * state[0] - single[3],
                )
                turned = (factor * applied[1], -factor * applied[0], factor * applied[3], -factor * applied[2])
                for c in range(4):
                    psi = state[c] if source is psi_ref else psi_ref[c, pl.ds(base + offset, 8), :]
                    value = psi + turned[c]
                    if target is None:
                        out_ref[pl.ds(row * 4 + c, 8, stride=4), :] = value
                    else:
                        write(target, c, plane, chunk, value)
            return carry

        lax.fori_loop(0, NX, body, 0)

    stage(4, psi_ref, ping_ref)
    stage(3, ping_ref, pong_ref)
    stage(2, pong_ref, ping_ref)
    stage(1, ping_ref, None)


def vmem(count):
    return [pl.BlockSpec(memory_space=pltpu.VMEM)] * count


def call(kernel, name, out_shapes, operands, scratch=(), in_specs=None, flops=0):
    moved = sum(math.prod(o.shape) * 4 for o in out_shapes) + sum(math.prod(o.shape) * 4 for o in operands)
    return pl.pallas_call(
        kernel,
        name=name,
        out_shape=[jax.ShapeDtypeStruct(o.shape, o.dtype) for o in out_shapes],
        in_specs=in_specs or vmem(len(operands)),
        out_specs=vmem(len(out_shapes)),
        scratch_shapes=[pltpu.VMEM(shape, F32) for shape in scratch],
        compiler_params=pltpu.CompilerParams(vmem_limit_bytes=56 * 1024 * 1024),
        cost_estimate=pl.CostEstimate(flops=flops, bytes_accessed=moved, transcendentals=0),
    )(*operands)


def like(*shape):
    return jax.ShapeDtypeStruct(shape, F32)


def local(quasi, outer_field, coupling):
    sizes = {name: lax.axis_size(name) for name in AXES}
    devices = sizes["grp"] * sizes["wf"]
    waves = quasi.shape[0]
    scale = 1.0 / (waves * devices)
    bits = [("grp", 1 << k) for k in range(1, sizes["grp"].bit_length() - 1)]
    bits += [("wf", 1 << k) for k in range(sizes["wf"].bit_length() - 1)]
    first, second, third, rest = bits[0], bits[1], bits[2], bits[3:]
    straight = [first, second, third] + rest
    crossed = [second, first, third] + rest
    real_plan = Plan(sizes, (straight, crossed), devices)
    imag_plan = Plan(sizes, (crossed, straight), devices)
    mean_plan = Plan(sizes, ([third, first, second] + rest, [third, second, first] + rest), min(devices, NG))
    tables = {name: jnp.asarray(table) for name, table in transform_tables().items()}

    def halves(plan):
        return [like(plan.pieces // 2, ROWS // plan.pieces, LANES)] * 2

    state = quasi.reshape(waves, 4, ROWS, LANES).transpose(0, 2, 1, 3).reshape(waves * ROWS * 4, LANES)
    outer_field = outer_field.reshape(ROWS, LANES)
    coupling = coupling.reshape(ROWS, LANES)

    real_own, real_other, imag_own, imag_other = call(
        functools.partial(kappa_kernel, (real_plan, imag_plan), waves, scale),
        "kappa", halves(real_plan) + halves(imag_plan), [state],
    )
    mean_own, mean_other = call(
        functools.partial(density_kernel, mean_plan, waves, scale),
        "density", halves(mean_plan), [state, tables["forward_y"], tables["forward_z"]], [(ROWS, LANES)],
    )
    real = reduce_scatter(real_plan, real_own, real_other)
    imag = reduce_scatter(imag_plan, imag_own, imag_other)
    mean = reduce_scatter(mean_plan, mean_own, mean_other)
    (spectrum,) = call(
        functools.partial(coulomb_kernel, mean_plan),
        "coulomb", [like(*mean[0].shape)],
        [*mean, tables["even"], tables["odd"], tables["symbol_xz"], tables["symbol_y"]],
        in_specs=vmem(5) + [pl.BlockSpec(memory_space=pltpu.SMEM)],
    )
    mean_parts = all_gather(mean_plan, spectrum)
    real_parts = all_gather(real_plan, real[0] + real[1])
    imag_parts = all_gather(imag_plan, imag[0] + imag[1])
    (mean_field,) = call(
        functools.partial(mean_kernel, mean_plan),
        "mean", [like(ROWS, LANES)],
        [*mean_parts, outer_field, tables["inverse_y"], tables["inverse_z"]], [(ROWS, LANES)],
    )

    padded = (4, NX * PADDED, LANES)
    evolved = []
    for wave in range(waves):
        own_state = state[wave * ROWS * 4 : (wave + 1) * ROWS * 4]
        evolved_rows, potentials = call(
            functools.partial(propagate_kernel, (real_plan, imag_plan)),
            "propagate",
            [like(ROWS * 4, LANES), like(3, NX // sizes["grp"], NG * NG // sizes["wf"])],
            [own_state, mean_field, coupling, *real_parts, *imag_parts],
            [(ROWS, LANES)] * 3 + [padded] * 3,
        )
        evolved.append(evolved_rows)
    evolved = jnp.concatenate(evolved) if waves > 1 else evolved[0]
    evolved = evolved.reshape(waves, ROWS, 4, LANES).transpose(0, 2, 1, 3).reshape(quasi.shape)
    return (evolved, potentials)


def solution(mesh):
    placed = (P(AXES, None, None), P(), P())
    return jax.shard_map(
        local,
        mesh=mesh,
        in_specs=placed,
        out_specs=(P(AXES, None, None), P(None, "grp", "wf")),
        check_vma=False,
    )
```

```python
import functools
import math

import jax
import jax.numpy as jnp
import numpy as np
from jax import lax
from jax.experimental import pallas as pl
from jax.experimental.pallas import tpu as pltpu
from jax.sharding import PartitionSpec as P

NX = 64
NG = 64
LANES = 2 * NG
PLANE = NG * NG // LANES
ROWS = NX * PLANE
AXES = ("grp", "wf")
GROUP = 4
ODD_AT = PLANE + 16
PADDED = ODD_AT + PLANE

time_step = 0.2
kinetic_coef = 0.5
density_coef = 1.0
coulomb_coef = 0.25

F32 = jnp.float32
BF16 = jnp.bfloat16


def fourier_basis(length):
    cells = np.arange(length)
    rows, waves = [np.ones(length) / math.sqrt(length)], [0]
    for wave in range(1, length // 2):
        angle = 2.0 * math.pi * (wave * cells % length) / length
        rows += [math.sqrt(2.0 / length) * np.cos(angle), math.sqrt(2.0 / length) * np.sin(angle)]
        waves += [wave, wave]
    rows.append(np.where(cells % 2 == 0, 1.0, -1.0) / math.sqrt(length))
    waves.append(length // 2)
    return np.stack(rows), np.array(waves)


def lattice_symbol(waves, length):
    return 2.0 - 2.0 * np.cos(2.0 * math.pi / length * waves)


def split(matrix):
    high = matrix.astype(np.float32).astype(jnp.bfloat16)
    low = (matrix - high.astype(np.float64)).astype(jnp.bfloat16)
    return np.stack([high, low])


def block_diagonal(matrix, count):
    return np.kron(np.eye(count), matrix)


def transform_tables():
    basis, waves = fourier_basis(NG)
    order = np.concatenate([np.arange(0, NG, 2), np.arange(1, NG, 2)])
    forward_y = block_diagonal(basis[:, order], GROUP)
    forward_z = block_diagonal(basis.T, 2)
    first, first_waves = fourier_basis(NX)
    even, odd = first_waves % 2 == 0, first_waves % 2 == 1
    symbol_x = lattice_symbol(first_waves, NX)
    symbol = lattice_symbol(waves, NG)
    symbol_xz = np.concatenate(
        [symbol_x[even][:, None] + symbol[None], symbol_x[odd][:, None] + symbol[None]], axis=1
    )
    ring = np.roll(np.eye(NG), 1, axis=1) + np.roll(np.eye(NG), -1, axis=1)
    depth = block_diagonal(ring, 2)
    return dict(
        depth=np.concatenate([depth, depth]).astype(jnp.bfloat16),
        forward_y=split(forward_y),
        forward_z=split(forward_z),
        inverse_y=split(forward_y.T),
        inverse_z=split(forward_z.T),
        even=first[even][:, : NX // 2].astype(np.float32),
        odd=first[odd][:, : NX // 2].astype(np.float32),
        symbol_xz=symbol_xz.astype(np.float32),
        symbol_y=symbol.astype(np.float32),
    )


class Plan:
    def __init__(self, sizes, orders, pieces):
        self.sizes = sizes
        self.orders = orders
        self.pieces = pieces
        self.halvings = int(math.log2(pieces)) - 1
        kept = [("grp", 1)] + sorted(orders[0][: self.halvings])
        assert kept[1:] == sorted(orders[1][: self.halvings])
        self.kept = kept

    def permutation(self, step):
        pairs = []
        for grp in range(self.sizes["grp"]):
            for wf in range(self.sizes["wf"]):
                axis, mask = ("grp", 1) if step < 0 else self.orders[grp & 1][step]
                to = (grp ^ mask, wf) if axis == "grp" else (grp, wf ^ mask)
                pairs.append((grp * self.sizes["wf"] + wf, to[0] * self.sizes["wf"] + to[1]))
        return pairs

    def identity(self, grp, wf):
        number = 0
        for place, (axis, mask) in enumerate(self.kept):
            value = grp if axis == "grp" else wf
            number = number + (((value >> int(math.log2(mask))) & 1) << place)
        return number

    def places(self, side):
        grp, wf = lax.axis_index("grp"), lax.axis_index("wf")
        core = (grp & 1) ^ side
        pieces = [self.identity(grp ^ side, wf)]
        for step in range(self.halvings):
            near, far = (
                self.identity(*[mask if axis == name else 0 for name in AXES])
                for axis, mask in (self.orders[0][step], self.orders[1][step])
            )
            flip = near + core * (far - near)
            pieces = [piece ^ turned for piece in pieces for turned in (0, flip)]
        return pieces


def reduce_scatter(plan, own, other):
    for step in range(-1, len(plan.orders[0])):
        received = lax.ppermute(other, AXES, plan.permutation(step))
        if step + 1 == len(plan.orders[0]):
            break
        if step + 1 < plan.halvings:
            half = own.shape[0] // 2
            own, other = own[:half] + received[:half], own[half:] + received[half:]
        else:
            own = own + received
            other = own
    return own, received


def all_gather(plan, piece):
    parts = [piece]
    for step in reversed(range(plan.halvings)):
        whole = parts[0] if len(parts) == 1 else jnp.concatenate(parts)
        parts = [whole, lax.ppermute(whole, AXES, plan.permutation(step))]
    return parts + [lax.ppermute(part, AXES, plan.permutation(-1)) for part in parts]


def lane(shape):
    return lax.broadcasted_iota(jnp.int32, shape, len(shape) - 1)


def swap(value):
    return pltpu.roll(value, NG, value.ndim - 1)


def cut(value):
    high = value.astype(BF16)
    return high, (value - high.astype(F32)).astype(BF16)


def product(left, right):
    return lax.dot_general(left, right, (((1,), (0,)), ((), ())), preferred_element_type=F32)


def times_table(value, table):
    high, low = cut(value)
    return product(high, table[0]) + (product(low, table[0]) + product(high, table[1]))


def table_times(table, value):
    high, low = cut(value)
    return product(table[0], high) + (product(table[0], low) + product(table[1], high))


def component(state_ref, wave, index, row, rows):
    return state_ref[pl.ds((wave * ROWS + row) * 4 + index, rows, stride=4), :]


def fold(near, far):
    low = lane(near.shape) < NG
    return jnp.where(low, near, swap(far)), jnp.where(low, swap(near), far)


def unfold(even, odd):
    low = lane(even.shape) < NG
    return jnp.where(low, even, swap(odd)), jnp.where(low, swap(even), odd)


def deal(plan, whole_ref, own_ref, other_ref):
    rows = ROWS // plan.pieces
    for side, out_ref in enumerate((own_ref, other_ref)):
        for index, piece in enumerate(plan.places(side)):
            out_ref[index] = whole_ref[pl.ds(pl.multiple_of(piece * rows, 8), rows), :]


def collect(plan, part_refs, whole_ref):
    rows = ROWS // plan.pieces
    for side in range(2):
        for index, piece in enumerate(plan.places(side)):
            part, at = divmod(index, plan.pieces // 4)
            whole_ref[pl.ds(pl.multiple_of(piece * rows, 8), rows), :] = part_refs[2 * side + part][at]


def kappa_kernel(plans, waves, scale, state_ref, *refs):
    out_refs, whole_refs = refs[:4], refs[4:]

    def kappa(plane):
        real = imag = None
        for wave in range(waves):
            u_real, u_imag, v_real, v_imag = (component(state_ref, wave, c, plane * PLANE, PLANE) for c in range(4))
            add_real = u_real * v_real + u_imag * v_imag
            add_imag = u_imag * v_real - u_real * v_imag
            real = add_real if real is None else real + add_real
            imag = add_imag if imag is None else imag + add_imag
        return real * scale, imag * scale

    def body(plane, carry):
        base = pl.multiple_of(plane * NG, 8)
        for near, far, whole_ref in zip(kappa(plane), kappa(plane + NX // 2), whole_refs):
            even, odd = fold(near, far)
            whole_ref[pl.ds(base, PLANE), :] = even
            whole_ref[pl.ds(base + PLANE, PLANE), :] = odd
        return carry

    lax.fori_loop(0, NX // 2, body, 0)
    for which, plan in enumerate(plans):
        deal(plan, whole_refs[which], out_refs[2 * which], out_refs[2 * which + 1])


def density_kernel(plan, waves, scale, state_ref, y_ref, z_ref, own_ref, other_ref, spectrum_ref):
    half = NX // 2

    def density(plane):
        total = None
        for wave in range(waves):
            real = component(state_ref, wave, 2, plane * PLANE, PLANE)
            imag = component(state_ref, wave, 3, plane * PLANE, PLANE)
            value = real * real + imag * imag
            total = value if total is None else total + value
        return total * scale

    def body(pair, carry):
        for group in (2 * pair, 2 * pair + 1):
            parts = []
            for j in range(GROUP):
                plane = group * GROUP + j
                parts += fold(density(plane), density(plane + half))
            value = times_table(jnp.concatenate(parts), z_ref)
            value = table_times(y_ref, value)
            for j in range(GROUP):
                spectrum_ref[pl.ds(group * GROUP + j, NG, stride=half), :] = value[j * NG : (j + 1) * NG]
        return carry

    lax.fori_loop(0, half // GROUP // 2, body, 0)
    deal(plan, spectrum_ref, own_ref, other_ref)


def coulomb_kernel(plan, own_ref, received_ref, even_ref, odd_ref, xz_ref, y_ref, out_ref):
    half = NX // 2
    low_lanes = lane((half, LANES)) < NG
    sign = jnp.where(low_lanes, 1.0, -1.0)
    count = ROWS // plan.pieces // half
    first = plan.identity(lax.axis_index("grp"), lax.axis_index("wf")) * count

    def dot(matrix, value, axis):
        return lax.dot_general(
            matrix, value, (((axis,), (0,)), ((), ())),
            precision=lax.Precision.HIGHEST, preferred_element_type=F32,
        )

    for k in range(count):
        rows = pl.ds(k * half, half)
        value = own_ref[0, rows, :] + received_ref[0, rows, :]
        value = swap(value) + sign * value
        value = jnp.where(low_lanes, dot(even_ref[...], value, 1), dot(odd_ref[...], value, 1))
        squared = xz_ref[...] + y_ref[first + k]
        kernel = jnp.where(
            squared > 0.001,
            4.0 * math.pi * coulomb_coef / jnp.where(squared > 0.001, squared, 1.0),
            0.0,
        )
        value = value * (density_coef + kernel)
        value = jnp.where(low_lanes, dot(even_ref[...], value, 0), dot(odd_ref[...], value, 0))
        out_ref[0, rows, :] = swap(value) + sign * value


def mean_kernel(plan, *refs):
    part_refs, (outer_ref, y_ref, z_ref, out_ref, spectrum_ref) = refs[:4], refs[4:]
    half = NX // 2
    collect(plan, part_refs, spectrum_ref)

    def body(pair, carry):
        for group in (2 * pair, 2 * pair + 1):
            value = jnp.concatenate(
                [spectrum_ref[pl.ds(group * GROUP + j, NG, stride=half), :] for j in range(GROUP)]
            )
            value = table_times(y_ref, value)
            value = times_table(value, z_ref)
            for j in range(GROUP):
                plane = group * GROUP + j
                near, far = (
                    outer_ref[pl.ds(pl.multiple_of(x * PLANE, 8), PLANE), :] for x in (plane, plane + half)
                )
                base = pl.multiple_of(plane * NG, 8)
                for part, outer in enumerate(fold(near, far)):
                    at = j * NG + part * PLANE
                    out_ref[pl.ds(base + part * PLANE, PLANE), :] = value[at : at + PLANE] + outer
        return carry

    lax.fori_loop(0, half // GROUP // 2, body, 0)


def propagate_kernel(plans, *refs):
    (state_ref, mean_ref, coupling_ref, depth_ref), refs = refs[:4], refs[4:]
    parts, refs = (refs[:4], refs[4:8]), refs[8:]
    out_ref, potentials_ref, single_ref, real_ref, imag_ref, depth_sum_ref = refs[:6]
    term_refs = refs[6:]
    half = NX // 2

    for plan, part_refs, pair_ref in zip(plans, parts, (real_ref, imag_ref)):
        collect(plan, part_refs, pair_ref)

    def write(ref, c, plane, part, chunk, value):
        base = pl.multiple_of((plane + 1) * PADDED, 8)
        if part == 0:
            ref[c, pl.ds(base + chunk * 8, 8), :] = value
            if chunk == 0:
                ref[c, pl.ds(base + PLANE, 1), :] = value[:1]
        else:
            ref[c, pl.ds(base + ODD_AT + chunk * 8, 8), :] = value
            if chunk == PLANE // 8 - 1:
                ref[c, pl.ds(base + ODD_AT - 1, 1), :] = value[7:]

    def close(ref):
        for source, target in ((0, half + 1), (half - 1, 0)):
            for c in range(4):
                for at in (0, ODD_AT):
                    value = ref[c, pl.ds((source + 1) * PADDED + at, PLANE), :]
                    ref[c, pl.ds(target * PADDED + at, PLANE), :] = swap(value)

    def prepare(plane, carry):
        for chunk in range(PLANE // 8):
            rows = [pl.multiple_of(x * PLANE + chunk * 8, 8) for x in (plane, plane + half)]
            folded = fold(*[coupling_ref[pl.ds(row, 8), :] for row in rows])
            for part in range(2):
                where = pl.ds(pl.multiple_of(plane * NG + part * PLANE + chunk * 8, 8), 8)
                single_ref[where, :] = 2.0 * mean_ref[where, :] + 12.0 * kinetic_coef
                real_ref[where, :] = -2.0 * folded[part] * real_ref[where, :]
                imag_ref[where, :] = -2.0 * folded[part] * imag_ref[where, :]
            for c in range(4):
                folded = fold(*[component(state_ref, 0, c, row, 8) for row in rows])
                for part in range(2):
                    write(term_refs[0], c, plane, part, chunk, folded[part])
        return carry

    lax.fori_loop(0, half, prepare, 0)
    close(term_refs[0])

    planes, width = potentials_ref.shape[1:]
    first = lax.axis_index("grp") * planes
    upper = first >= half
    start = (first - jnp.where(upper, half, 0)) * NG + lax.axis_index("wf") * (width // LANES)
    low = lane((planes, LANES)) < NG
    for which, (ref, factor) in enumerate(((mean_ref, 1.0), (real_ref, 0.5), (imag_ref, 0.5))):
        for j in range(width // LANES):
            even = ref[pl.ds(start + j, planes, stride=NG), :]
            odd = ref[pl.ds(start + PLANE + j, planes, stride=NG), :]
            near, far = unfold(even, odd)
            potentials_ref[which, :, j * LANES : (j + 1) * LANES] = factor * jnp.where(upper, far, near)

    def depth_sums(source, plane, slot):
        base = pl.multiple_of((plane + 1) * PADDED, 8)
        value = jnp.concatenate([source[c, pl.ds(base + at, PLANE), :] for c in range(4) for at in (0, ODD_AT)])
        depth_sum_ref[slot] = product(jnp.concatenate(cut(value), axis=1), depth_ref[...])

    def finish(source, target, plane, slot):
        base = pl.multiple_of((plane + 1) * PADDED, 8)
        for part in range(2):
            for chunk in range(PLANE // 8):
                at = chunk * 8 + part * ODD_AT
                across = chunk * 8 + (1 - part) * ODD_AT
                beyond = across - 1 if part == 0 else across + 1
                where = pl.ds(pl.multiple_of(plane * NG + part * PLANE + chunk * 8, 8), 8)
                single, real, imag = single_ref[where, :], real_ref[where, :], imag_ref[where, :]
                state, total = [], []
                for c in range(4):
                    state.append(source[c, pl.ds(base + at, 8), :])
                    total.append(
                        (source[c, pl.ds(base - PADDED + at, 8), :] + source[c, pl.ds(base + PADDED + at, 8), :])
                        + (source[c, pl.ds(base + across, 8), :] + source[c, pl.ds(base + beyond, 8), :])
                        + depth_sum_ref[slot, pl.ds(c * NG + part * PLANE + chunk * 8, 8), :]
                    )
                values = (
                    (single * state[1] - total[1]) + (real * state[3] + imag * state[2]),
                    (total[0] - single * state[0]) + (imag * state[3] - real * state[2]),
                    (total[3] - single * state[3]) + (real * state[1] - imag * state[0]),
                    (single * state[2] - total[2]) - (real * state[0] + imag * state[1]),
                )
                if target is not None:
                    for c in range(4):
                        write(target, c, plane, part, chunk, values[c])
                    continue
                for c in range(4):
                    result = values[c] * weights[4] + state[c] * weights[3]
                    for k in (2, 1):
                        result = result + term_refs[k][c, pl.ds(base + at, 8), :] * weights[k]
                    results[part][chunk][c] = result + term_refs[0][c, pl.ds(base + at, 8), :]
        if target is None:
            for chunk in range(PLANE // 8):
                for c in range(4):
                    folded = unfold(results[0][chunk][c], results[1][chunk][c])
                    for x, value in zip((plane, plane + half), folded):
                        out_ref[pl.ds((x * PLANE + chunk * 8) * 4 + c, 8, stride=4), :] = value

    weights = [(0.5 * time_step) ** k / math.factorial(k) for k in range(5)]
    results = [[[None] * 4 for _ in range(PLANE // 8)] for _ in range(2)]
    for source, target in zip(term_refs, list(term_refs[1:]) + [None]):
        depth_sums(source, 0, 0)

        def body(pair, carry, source=source, target=target):
            for slot in range(2):
                finish(source, target, 2 * pair + slot, slot)
                depth_sums(source, 2 * pair + slot + 1, 1 - slot)
            return carry

        lax.fori_loop(0, half // 2, body, 0)
        if target is not None:
            close(target)


def vmem(count):
    return [pl.BlockSpec(memory_space=pltpu.VMEM)] * count


def call(kernel, name, out_shapes, operands, scratch=(), in_specs=None, flops=0):
    moved = sum(math.prod(o.shape) * 4 for o in out_shapes) + sum(math.prod(o.shape) * 4 for o in operands)
    return pl.pallas_call(
        kernel,
        name=name,
        out_shape=[jax.ShapeDtypeStruct(o.shape, o.dtype) for o in out_shapes],
        in_specs=in_specs or vmem(len(operands)),
        out_specs=vmem(len(out_shapes)),
        scratch_shapes=[pltpu.VMEM(shape, F32) for shape in scratch],
        compiler_params=pltpu.CompilerParams(vmem_limit_bytes=56 * 1024 * 1024),
        cost_estimate=pl.CostEstimate(flops=flops, bytes_accessed=moved, transcendentals=0),
    )(*operands)


def like(*shape):
    return jax.ShapeDtypeStruct(shape, F32)


def local(quasi, outer_field, coupling):
    sizes = {name: lax.axis_size(name) for name in AXES}
    devices = sizes["grp"] * sizes["wf"]
    waves = quasi.shape[0]
    scale = 1.0 / (waves * devices)
    bits = [("grp", 1 << k) for k in range(1, sizes["grp"].bit_length() - 1)]
    bits += [("wf", 1 << k) for k in range(sizes["wf"].bit_length() - 1)]
    first, second, third, rest = bits[0], bits[1], bits[2], bits[3:]
    straight = [first, second, third] + rest
    crossed = [second, first, third] + rest
    real_plan = Plan(sizes, (straight, crossed), devices)
    imag_plan = Plan(sizes, (crossed, straight), devices)
    mean_plan = Plan(sizes, ([third, first, second] + rest, [third, second, first] + rest), min(devices, NG))
    tables = {name: jnp.asarray(table) for name, table in transform_tables().items()}

    def halves(plan):
        return [like(plan.pieces // 2, ROWS // plan.pieces, LANES)] * 2

    state = quasi.reshape(waves, 4, ROWS, LANES).transpose(0, 2, 1, 3).reshape(waves * ROWS * 4, LANES)
    outer_field = outer_field.reshape(ROWS, LANES)
    coupling = coupling.reshape(ROWS, LANES)

    real_own, real_other, imag_own, imag_other = call(
        functools.partial(kappa_kernel, (real_plan, imag_plan), waves, scale),
        "kappa", halves(real_plan) + halves(imag_plan), [state], [(ROWS, LANES)] * 2,
    )
    mean_own, mean_other = call(
        functools.partial(density_kernel, mean_plan, waves, scale),
        "density", halves(mean_plan), [state, tables["forward_y"], tables["forward_z"]], [(ROWS, LANES)],
    )
    real = reduce_scatter(real_plan, real_own, real_other)
    imag = reduce_scatter(imag_plan, imag_own, imag_other)
    mean = reduce_scatter(mean_plan, mean_own, mean_other)
    (spectrum,) = call(
        functools.partial(coulomb_kernel, mean_plan),
        "coulomb", [like(*mean[0].shape)],
        [*mean, tables["even"], tables["odd"], tables["symbol_xz"], tables["symbol_y"]],
        in_specs=vmem(5) + [pl.BlockSpec(memory_space=pltpu.SMEM)],
    )
    mean_parts = all_gather(mean_plan, spectrum)
    real_parts = all_gather(real_plan, real[0] + real[1])
    imag_parts = all_gather(imag_plan, imag[0] + imag[1])
    (mean_field,) = call(
        functools.partial(mean_kernel, mean_plan),
        "mean", [like(ROWS, LANES)],
        [*mean_parts, outer_field, tables["inverse_y"], tables["inverse_z"]], [(ROWS, LANES)],
    )

    padded = (4, (NX // 2 + 2) * PADDED, LANES)
    evolved = []
    for wave in range(waves):
        own_state = state[wave * ROWS * 4 : (wave + 1) * ROWS * 4]
        evolved_rows, potentials = call(
            functools.partial(propagate_kernel, (real_plan, imag_plan)),
            "propagate",
            [like(ROWS * 4, LANES), like(3, NX // sizes["grp"], NG * NG // sizes["wf"])],
            [own_state, mean_field, coupling, tables["depth"], *real_parts, *imag_parts],
            [(ROWS, LANES)] * 3 + [(2, 4 * NG, LANES)] + [padded] * 4,
        )
        evolved.append(evolved_rows)
    evolved = jnp.concatenate(evolved) if waves > 1 else evolved[0]
    evolved = evolved.reshape(waves, ROWS, 4, LANES).transpose(0, 2, 1, 3).reshape(quasi.shape)
    return (evolved, potentials)


def solution(mesh):
    placed = (P(AXES, None, None), P(), P())
    return jax.shard_map(
        local,
        mesh=mesh,
        in_specs=placed,
        out_specs=(P(AXES, None, None), P(None, "grp", "wf")),
        check_vma=False,
    )
```

```python
import functools
import math

import jax
import jax.numpy as jnp
import numpy as np
from jax import lax
from jax.experimental import pallas as pl
from jax.experimental.pallas import tpu as pltpu
from jax.sharding import PartitionSpec as P

NX = 64
NG = 64
LANES = 2 * NG
PLANE = NG * NG // LANES
ROWS = NX * PLANE
AXES = ("grp", "wf")
GROUP = 4
PAD = 8
PADDED = PLANE + 2 * PAD
STEP = 2
CHUNKS = 8

time_step = 0.2
kinetic_coef = 0.5
density_coef = 1.0
coulomb_coef = 0.25

F32 = jnp.float32
BF16 = jnp.bfloat16


def fourier_basis(length):
    cells = np.arange(length)
    rows, waves = [np.ones(length) / math.sqrt(length)], [0]
    for wave in range(1, length // 2):
        angle = 2.0 * math.pi * (wave * cells % length) / length
        rows += [math.sqrt(2.0 / length) * np.cos(angle), math.sqrt(2.0 / length) * np.sin(angle)]
        waves += [wave, wave]
    rows.append(np.where(cells % 2 == 0, 1.0, -1.0) / math.sqrt(length))
    waves.append(length // 2)
    return np.stack(rows), np.array(waves)


def lattice_symbol(waves, length):
    return 2.0 - 2.0 * np.cos(2.0 * math.pi / length * waves)


def split(matrix):
    high = matrix.astype(np.float32).astype(jnp.bfloat16)
    low = (matrix - high.astype(np.float64)).astype(jnp.bfloat16)
    return np.stack([high, low])


def block_diagonal(matrix, count):
    return np.kron(np.eye(count), matrix)


def transform_tables():
    basis, waves = fourier_basis(NG)
    order = np.concatenate([np.arange(0, NG, 2), np.arange(1, NG, 2)])
    forward_y = block_diagonal(basis[:, order], GROUP)
    forward_z = block_diagonal(basis.T, 2)
    first, first_waves = fourier_basis(NX)
    even, odd = first_waves % 2 == 0, first_waves % 2 == 1
    symbol_x = lattice_symbol(first_waves, NX)
    symbol = lattice_symbol(waves, NG)
    symbol_xz = np.concatenate(
        [symbol_x[even][:, None] + symbol[None], symbol_x[odd][:, None] + symbol[None]], axis=1
    )
    ring = np.roll(np.eye(NG), 1, axis=1) + np.roll(np.eye(NG), -1, axis=1)
    swapped = np.roll(np.eye(LANES), NG, axis=1)
    shift = np.concatenate([block_diagonal(ring, 2) + swapped, swapped], axis=1)
    return dict(
        shift=np.concatenate([shift, shift]).astype(jnp.bfloat16),
        forward_y=split(forward_y),
        forward_z=split(forward_z),
        inverse_y=split(forward_y.T),
        inverse_z=split(forward_z.T),
        even=first[even][:, : NX // 2].astype(np.float32),
        odd=first[odd][:, : NX // 2].astype(np.float32),
        symbol_xz=symbol_xz.astype(np.float32),
        symbol_y=symbol.astype(np.float32),
    )


class Plan:
    def __init__(self, sizes, orders, pieces):
        self.sizes = sizes
        self.orders = orders
        self.pieces = pieces
        self.halvings = int(math.log2(pieces)) - 1
        kept = [("grp", 1)] + sorted(orders[0][: self.halvings])
        assert kept[1:] == sorted(orders[1][: self.halvings])
        self.kept = kept

    def permutation(self, step):
        pairs = []
        for grp in range(self.sizes["grp"]):
            for wf in range(self.sizes["wf"]):
                axis, mask = ("grp", 1) if step < 0 else self.orders[grp & 1][step]
                to = (grp ^ mask, wf) if axis == "grp" else (grp, wf ^ mask)
                pairs.append((grp * self.sizes["wf"] + wf, to[0] * self.sizes["wf"] + to[1]))
        return pairs

    def identity(self, grp, wf):
        number = 0
        for place, (axis, mask) in enumerate(self.kept):
            value = grp if axis == "grp" else wf
            number = number + (((value >> int(math.log2(mask))) & 1) << place)
        return number

    def places(self, side):
        grp, wf = lax.axis_index("grp"), lax.axis_index("wf")
        core = (grp & 1) ^ side
        pieces = [self.identity(grp ^ side, wf)]
        for step in range(self.halvings):
            near, far = (
                self.identity(*[mask if axis == name else 0 for name in AXES])
                for axis, mask in (self.orders[0][step], self.orders[1][step])
            )
            flip = near + core * (far - near)
            pieces = [piece ^ turned for piece in pieces for turned in (0, flip)]
        return pieces


def reduce_scatter(plan, own, other):
    for step in range(-1, len(plan.orders[0])):
        received = lax.ppermute(other, AXES, plan.permutation(step))
        if step + 1 == len(plan.orders[0]):
            break
        if step + 1 < plan.halvings:
            half = own.shape[0] // 2
            own, other = own[:half] + received[:half], own[half:] + received[half:]
        else:
            own = own + received
            other = own
    return own, received


def all_gather(plan, piece):
    parts = [piece]
    for step in reversed(range(plan.halvings)):
        whole = parts[0] if len(parts) == 1 else jnp.concatenate(parts)
        parts = [whole, lax.ppermute(whole, AXES, plan.permutation(step))]
    return parts + [lax.ppermute(part, AXES, plan.permutation(-1)) for part in parts]


def lane(shape):
    return lax.broadcasted_iota(jnp.int32, shape, len(shape) - 1)


def swap(value):
    return pltpu.roll(value, NG, value.ndim - 1)


def cut(value):
    high = value.astype(BF16)
    return high, (value - high.astype(F32)).astype(BF16)


def product(left, right):
    return lax.dot_general(left, right, (((1,), (0,)), ((), ())), preferred_element_type=F32)


def times_table(value, table):
    high, low = cut(value)
    return product(high, table[0]) + (product(low, table[0]) + product(high, table[1]))


def table_times(table, value):
    high, low = cut(value)
    return product(table[0], high) + (product(table[0], low) + product(table[1], high))


def fold(near, far):
    low = lane(near.shape) < NG
    return jnp.where(low, near, swap(far)), jnp.where(low, swap(near), far)


def unfold(even, odd):
    low = lane(even.shape) < NG
    return jnp.where(low, even, swap(odd)), jnp.where(low, swap(even), odd)


def deal(plan, whole_ref, own_ref, other_ref):
    rows = ROWS // plan.pieces
    for side, out_ref in enumerate((own_ref, other_ref)):
        for index, piece in enumerate(plan.places(side)):
            out_ref[index] = whole_ref[pl.ds(pl.multiple_of(piece * rows, 8), rows), :]


def collect(plan, part_refs, store):
    rows = ROWS // plan.pieces
    for side in range(2):
        for index, piece in enumerate(plan.places(side)):
            part, at = divmod(index, plan.pieces // 4)
            store(pl.ds(pl.multiple_of(piece * rows, 8), rows), part_refs[2 * side + part][at])


def kappa_kernel(plans, scale, state_ref, *refs):
    out_refs, psi_ref, whole_refs, arrived = refs[:4], refs[4], refs[5:7], refs[7]
    waves, rows = psi_ref.shape[0], ROWS // CHUNKS
    copies = [
        [
            pltpu.make_async_copy(
                state_ref.at[wave, pl.ds(chunk * rows, rows), c, :],
                psi_ref.at[wave, c, pl.ds(chunk * rows, rows), :],
                arrived.at[chunk, wave, c],
            )
            for wave in range(waves)
            for c in range(4)
        ]
        for chunk in range(CHUNKS)
    ]
    for chunk in copies:
        for copy in chunk:
            copy.start()

    for chunk in range(CHUNKS):
        for copy in copies[chunk]:
            copy.wait()

        def body(plane, carry, chunk=chunk):
            where = pl.ds(pl.multiple_of(chunk * rows + plane * PLANE, 8), PLANE)
            real = imag = None
            for wave in range(waves):
                u_real, u_imag, v_real, v_imag = (psi_ref[wave, c, where, :] for c in range(4))
                add_real = u_real * v_real + u_imag * v_imag
                add_imag = u_imag * v_real - u_real * v_imag
                real = add_real if real is None else real + add_real
                imag = add_imag if imag is None else imag + add_imag
            whole_refs[0][where, :] = real * scale
            whole_refs[1][where, :] = imag * scale
            return carry

        lax.fori_loop(0, rows // PLANE, body, 0)
    for which, plan in enumerate(plans):
        deal(plan, whole_refs[which], out_refs[2 * which], out_refs[2 * which + 1])


def density_kernel(plan, scale, psi_ref, y_ref, z_ref, own_ref, other_ref, spectrum_ref):
    half = NX // 2

    def density(plane):
        where = pl.ds(pl.multiple_of(plane * PLANE, 8), PLANE)
        total = None
        for wave in range(psi_ref.shape[0]):
            real, imag = psi_ref[wave, 2, where, :], psi_ref[wave, 3, where, :]
            value = real * real + imag * imag
            total = value if total is None else total + value
        return total * scale

    def body(pair, carry):
        for group in (2 * pair, 2 * pair + 1):
            parts = []
            for j in range(GROUP):
                plane = group * GROUP + j
                parts += fold(density(plane), density(plane + half))
            value = times_table(jnp.concatenate(parts), z_ref)
            value = table_times(y_ref, value)
            for j in range(GROUP):
                spectrum_ref[pl.ds(group * GROUP + j, NG, stride=half), :] = value[j * NG : (j + 1) * NG]
        return carry

    lax.fori_loop(0, half // GROUP // 2, body, 0)
    deal(plan, spectrum_ref, own_ref, other_ref)


def coulomb_kernel(plan, own_ref, received_ref, even_ref, odd_ref, xz_ref, y_ref, out_ref):
    half = NX // 2
    low_lanes = lane((half, LANES)) < NG
    sign = jnp.where(low_lanes, 1.0, -1.0)
    count = ROWS // plan.pieces // half
    first = plan.identity(lax.axis_index("grp"), lax.axis_index("wf")) * count

    def dot(matrix, value, axis):
        return lax.dot_general(
            matrix, value, (((axis,), (0,)), ((), ())),
            precision=lax.Precision.HIGHEST, preferred_element_type=F32,
        )

    for k in range(count):
        rows = pl.ds(k * half, half)
        value = own_ref[0, rows, :] + received_ref[0, rows, :]
        value = swap(value) + sign * value
        value = jnp.where(low_lanes, dot(even_ref[...], value, 1), dot(odd_ref[...], value, 1))
        squared = xz_ref[...] + y_ref[first + k]
        kernel = jnp.where(
            squared > 0.001,
            4.0 * math.pi * coulomb_coef / jnp.where(squared > 0.001, squared, 1.0),
            0.0,
        )
        value = value * (density_coef + kernel)
        value = jnp.where(low_lanes, dot(even_ref[...], value, 0), dot(odd_ref[...], value, 0))
        out_ref[0, rows, :] = swap(value) + sign * value


def mean_kernel(plan, *refs):
    part_refs, (outer_ref, y_ref, z_ref, out_ref, spectrum_ref) = refs[:4], refs[4:]
    half = NX // 2

    def store(where, value):
        spectrum_ref[where, :] = value

    collect(plan, part_refs, store)

    def body(pair, carry):
        for group in (2 * pair, 2 * pair + 1):
            value = jnp.concatenate(
                [spectrum_ref[pl.ds(group * GROUP + j, NG, stride=half), :] for j in range(GROUP)]
            )
            value = table_times(y_ref, value)
            value = times_table(value, z_ref)
            for j in range(GROUP):
                at = j * NG
                natural = unfold(value[at : at + PLANE], value[at + PLANE : at + NG])
                for x, part in zip((group * GROUP + j, group * GROUP + j + half), natural):
                    where = pl.ds(pl.multiple_of(x * PLANE, 8), PLANE)
                    out_ref[where, :] = part + outer_ref[where, :]
        return carry

    lax.fori_loop(0, half // GROUP // 2, body, 0)


def propagate_kernel(plans, *refs):
    (psi_ref, mean_ref, coupling_ref, shift_ref), refs = refs[:4], refs[4:]
    parts, refs = (refs[:4], refs[4:8]), refs[8:]
    out_ref, potentials_ref, single_ref, real_ref, imag_ref, inner_ref, swapped_ref = refs[:7]
    (*buffers, left) = refs[7:]
    terms = [psi_ref.at[0]] + buffers

    for plan, part_refs, pair_ref in zip(plans, parts, (real_ref, imag_ref)):

        def store(where, value, pair_ref=pair_ref):
            pair_ref[where, :] = -2.0 * coupling_ref[where, :] * value

        collect(plan, part_refs, store)

    def prepare(plane, carry):
        where = pl.ds(pl.multiple_of(plane * PLANE, 8), PLANE)
        single_ref[where, :] = 2.0 * mean_ref[where, :] + 12.0 * kinetic_coef
        return carry

    lax.fori_loop(0, NX, prepare, 0)

    planes, width = potentials_ref.shape[1:]
    start = lax.axis_index("grp") * planes * PLANE + lax.axis_index("wf") * (width // LANES)
    for which, (ref, factor) in enumerate(((mean_ref, 1.0), (real_ref, 0.5), (imag_ref, 0.5))):
        for j in range(width // LANES):
            value = ref[pl.ds(start + j, planes, stride=PLANE), :]
            potentials_ref[which, :, j * LANES : (j + 1) * LANES] = factor * value

    low_lanes = lane((8, LANES)) < NG

    def in_lanes(source, first, slot):
        value = jnp.concatenate(
            [
                source[c, pl.ds(pl.multiple_of((first + p) * PLANE, 8), PLANE), :]
                for p in range(STEP)
                for c in range(4)
            ]
        )
        moved = product(jnp.concatenate(cut(value), axis=1), shift_ref[...])
        inner_ref[slot] = moved[:, :LANES]
        for k in range(4 * STEP):
            rows = moved[k * PLANE : (k + 1) * PLANE, LANES:]
            swapped_ref[slot, k, PAD : PAD + PLANE] = rows
            swapped_ref[slot, k, PAD - 1 : PAD] = rows[PLANE - 1 :]
            swapped_ref[slot, k, PAD + PLANE : PAD + PLANE + 1] = rows[:1]

    weights = [(0.5 * time_step) ** k / math.factorial(k) for k in range(5)]

    def finish(source, target, plane, p, slot):
        base = pl.multiple_of(plane * PLANE, 8)
        before = pl.multiple_of(((plane + NX - 1) & (NX - 1)) * PLANE, 8)
        after = pl.multiple_of(((plane + 1) & (NX - 1)) * PLANE, 8)
        for chunk in range(PLANE // 8):
            where = pl.ds(base + chunk * 8, 8)
            single, real, imag = single_ref[where, :], real_ref[where, :], imag_ref[where, :]
            state, total = [], []
            for c in range(4):
                k = p * 4 + c
                at = PAD + chunk * 8
                state.append(source[c, where, :])
                total.append(
                    (source[c, pl.ds(before + chunk * 8, 8), :] + source[c, pl.ds(after + chunk * 8, 8), :])
                    + (
                        inner_ref[slot, k * PLANE + chunk * 8 : k * PLANE + chunk * 8 + 8]
                        + jnp.where(
                            low_lanes,
                            swapped_ref[slot, k, at - 1 : at + 7],
                            swapped_ref[slot, k, at + 1 : at + 9],
                        )
                    )
                )
            values = (
                (single * state[1] - total[1]) + (real * state[3] + imag * state[2]),
                (total[0] - single * state[0]) + (imag * state[3] - real * state[2]),
                (total[3] - single * state[3]) + (real * state[1] - imag * state[0]),
                (single * state[2] - total[2]) - (real * state[0] + imag * state[1]),
            )
            for c in range(4):
                value = values[c]
                if target is None:
                    value = value * weights[4] + state[c] * weights[3]
                    for k in (2, 1):
                        value = value + terms[k][c, where, :] * weights[k]
                    terms[1][c, where, :] = value + terms[0][c, where, :]
                else:
                    target[c, where, :] = value

    block = 2 * STEP

    def leave(index, c):
        where = pl.ds(pl.multiple_of(index * (block * PLANE), 8), block * PLANE)
        return pltpu.make_async_copy(terms[1].at[c, where, :], out_ref.at[where, c, :], left.at[index, c])

    for source, target in zip(terms, terms[1:] + [None]):
        in_lanes(source, 0, 0)

        def body(index, carry, source=source, target=target):
            for slot in range(2):
                first = index * block + slot * STEP
                for p in range(STEP):
                    finish(source, target, first + p, p, slot)
                in_lanes(source, (first + STEP) & (NX - 1), 1 - slot)
            if target is None:
                for c in range(4):
                    leave(index, c).start()
            return carry

        lax.fori_loop(0, NX // block, body, 0)
    for index in range(NX // block):
        for c in range(4):
            leave(index, c).wait()


VMEM = pl.BlockSpec(memory_space=pltpu.VMEM)
ANY = pl.BlockSpec(memory_space=pl.ANY)
SMEM = pl.BlockSpec(memory_space=pltpu.SMEM)


def call(kernel, name, out_shapes, operands, scratch=(), in_specs=None, out_specs=None, limit=16):
    moved = sum(math.prod(o.shape) * 4 for o in (*out_shapes, *operands))
    return pl.pallas_call(
        kernel,
        name=name,
        out_shape=[jax.ShapeDtypeStruct(o.shape, o.dtype) for o in out_shapes],
        in_specs=in_specs or [VMEM] * len(operands),
        out_specs=out_specs or [VMEM] * len(out_shapes),
        scratch_shapes=[pltpu.VMEM(s, F32) if isinstance(s, tuple) else s for s in scratch],
        compiler_params=pltpu.CompilerParams(vmem_limit_bytes=limit * 1024 * 1024),
        cost_estimate=pl.CostEstimate(flops=0, bytes_accessed=moved, transcendentals=0),
    )(*operands)


def like(*shape):
    return jax.ShapeDtypeStruct(shape, F32)


def local(quasi, outer_field, coupling):
    sizes = {name: lax.axis_size(name) for name in AXES}
    devices = sizes["grp"] * sizes["wf"]
    waves = quasi.shape[0]
    scale = 1.0 / (waves * devices)
    bits = [("grp", 1 << k) for k in range(1, sizes["grp"].bit_length() - 1)]
    bits += [("wf", 1 << k) for k in range(sizes["wf"].bit_length() - 1)]
    first, second, third, rest = bits[0], bits[1], bits[2], bits[3:]
    straight = [first, second, third] + rest
    crossed = [second, first, third] + rest
    real_plan = Plan(sizes, (straight, crossed), devices)
    imag_plan = Plan(sizes, (crossed, straight), devices)
    mean_plan = Plan(sizes, ([third, first, second] + rest, [third, second, first] + rest), min(devices, NG))
    tables = {name: jnp.asarray(table) for name, table in transform_tables().items()}

    def halves(plan):
        return [like(plan.pieces // 2, ROWS // plan.pieces, LANES)] * 2

    state = quasi.reshape(waves, 4, ROWS, LANES).transpose(0, 2, 1, 3)
    outer_field = outer_field.reshape(ROWS, LANES)
    coupling = coupling.reshape(ROWS, LANES)

    real_own, real_other, imag_own, imag_other, psi = call(
        functools.partial(kappa_kernel, (real_plan, imag_plan), scale),
        "kappa", halves(real_plan) + halves(imag_plan) + [like(waves, 4, ROWS, LANES)], [state],
        [(ROWS, LANES)] * 2 + [pltpu.SemaphoreType.DMA((CHUNKS, waves, 4))], in_specs=[ANY],
    )
    mean_own, mean_other = call(
        functools.partial(density_kernel, mean_plan, scale),
        "density", halves(mean_plan), [psi, tables["forward_y"], tables["forward_z"]], [(ROWS, LANES)],
    )
    real = reduce_scatter(real_plan, real_own, real_other)
    imag = reduce_scatter(imag_plan, imag_own, imag_other)
    mean = reduce_scatter(mean_plan, mean_own, mean_other)
    (spectrum,) = call(
        functools.partial(coulomb_kernel, mean_plan),
        "coulomb", [like(*mean[0].shape)],
        [*mean, tables["even"], tables["odd"], tables["symbol_xz"], tables["symbol_y"]],
        in_specs=[VMEM] * 5 + [SMEM],
    )
    mean_parts = all_gather(mean_plan, spectrum)
    real_parts = all_gather(real_plan, real[0] + real[1])
    imag_parts = all_gather(imag_plan, imag[0] + imag[1])
    (mean_field,) = call(
        functools.partial(mean_kernel, mean_plan),
        "mean", [like(ROWS, LANES)],
        [*mean_parts, outer_field, tables["inverse_y"], tables["inverse_z"]], [(ROWS, LANES)],
    )

    evolved = []
    for wave in range(waves):
        evolved_rows, potentials = call(
            functools.partial(propagate_kernel, (real_plan, imag_plan)),
            "propagate",
            [like(ROWS, 4, LANES), like(3, NX // sizes["grp"], NG * NG // sizes["wf"])],
            [psi[wave : wave + 1], mean_field, coupling, tables["shift"], *real_parts, *imag_parts],
            [(ROWS, LANES)] * 3
            + [(2, 4 * STEP * PLANE, LANES), (2, 4 * STEP, PADDED, LANES)]
            + [(4, ROWS, LANES)] * 3
            + [pltpu.SemaphoreType.DMA((NX // (2 * STEP), 4))],
            out_specs=[ANY, VMEM],
            limit=32,
        )
        evolved.append(evolved_rows)
    evolved = jnp.stack(evolved) if waves > 1 else evolved[0][None]
    evolved = evolved.transpose(0, 2, 1, 3).reshape(quasi.shape)
    return (evolved, potentials)


def solution(mesh):
    placed = (P(AXES, None, None), P(), P())
    return jax.shard_map(
        local,
        mesh=mesh,
        in_specs=placed,
        out_specs=(P(AXES, None, None), P(None, "grp", "wf")),
        check_vma=False,
    )
```

```python
import functools
import math

import jax
import jax.numpy as jnp
import numpy as np
from jax import lax
from jax.experimental import pallas as pl
from jax.experimental.pallas import tpu as pltpu
from jax.sharding import PartitionSpec as P

NX = 64
NG = 64
LANES = 2 * NG
PLANE = NG * NG // LANES
ROWS = NX * PLANE
AXES = ("grp", "wf")
GROUP = 4
PAD = 8
PADDED = PLANE + 2 * PAD
STEP = 4
SLOTS = 2
AHEAD = 1
FLAGS = None
CHUNKS = 8

time_step = 0.2
kinetic_coef = 0.5
density_coef = 1.0
coulomb_coef = 0.25

F32 = jnp.float32
BF16 = jnp.bfloat16


def fourier_basis(length):
    cells = np.arange(length)
    rows, waves = [np.ones(length) / math.sqrt(length)], [0]
    for wave in range(1, length // 2):
        angle = 2.0 * math.pi * (wave * cells % length) / length
        rows += [math.sqrt(2.0 / length) * np.cos(angle), math.sqrt(2.0 / length) * np.sin(angle)]
        waves += [wave, wave]
    rows.append(np.where(cells % 2 == 0, 1.0, -1.0) / math.sqrt(length))
    waves.append(length // 2)
    return np.stack(rows), np.array(waves)


def lattice_symbol(waves, length):
    return 2.0 - 2.0 * np.cos(2.0 * math.pi / length * waves)


def split(matrix):
    high = matrix.astype(np.float32).astype(jnp.bfloat16)
    low = (matrix - high.astype(np.float64)).astype(jnp.bfloat16)
    return np.stack([high, low])


def block_diagonal(matrix, count):
    return np.kron(np.eye(count), matrix)


def transform_tables():
    basis, waves = fourier_basis(NG)
    order = np.concatenate([np.arange(0, NG, 2), np.arange(1, NG, 2)])
    forward_y = block_diagonal(basis[:, order], GROUP)
    forward_z = block_diagonal(basis.T, 2)
    first, first_waves = fourier_basis(NX)
    even, odd = first_waves % 2 == 0, first_waves % 2 == 1
    symbol_x = lattice_symbol(first_waves, NX)
    symbol = lattice_symbol(waves, NG)
    symbol_xz = np.concatenate(
        [symbol_x[even][:, None] + symbol[None], symbol_x[odd][:, None] + symbol[None]], axis=1
    )
    ring = np.roll(np.eye(NG), 1, axis=1) + np.roll(np.eye(NG), -1, axis=1)
    swapped = np.roll(np.eye(LANES), NG, axis=1)
    shift = np.concatenate([block_diagonal(ring, 2) + swapped, swapped], axis=1)
    return dict(
        shift=np.concatenate([shift, shift]).astype(jnp.bfloat16),
        forward_y=split(forward_y),
        forward_z=split(forward_z),
        inverse_y=split(forward_y.T),
        inverse_z=split(forward_z.T),
        even=first[even][:, : NX // 2].astype(np.float32),
        odd=first[odd][:, : NX // 2].astype(np.float32),
        symbol_xz=symbol_xz.astype(np.float32),
        symbol_y=symbol.astype(np.float32),
    )


class Plan:
    def __init__(self, sizes, orders, pieces):
        self.sizes = sizes
        self.orders = orders
        self.pieces = pieces
        self.halvings = int(math.log2(pieces)) - 1
        kept = [("grp", 1)] + sorted(orders[0][: self.halvings])
        assert kept[1:] == sorted(orders[1][: self.halvings])
        self.kept = kept

    def permutation(self, step):
        pairs = []
        for grp in range(self.sizes["grp"]):
            for wf in range(self.sizes["wf"]):
                axis, mask = ("grp", 1) if step < 0 else self.orders[grp & 1][step]
                to = (grp ^ mask, wf) if axis == "grp" else (grp, wf ^ mask)
                pairs.append((grp * self.sizes["wf"] + wf, to[0] * self.sizes["wf"] + to[1]))
        return pairs

    def identity(self, grp, wf):
        number = 0
        for place, (axis, mask) in enumerate(self.kept):
            value = grp if axis == "grp" else wf
            number = number + (((value >> int(math.log2(mask))) & 1) << place)
        return number

    def places(self, side):
        grp, wf = lax.axis_index("grp"), lax.axis_index("wf")
        core = (grp & 1) ^ side
        pieces = [self.identity(grp ^ side, wf)]
        for step in range(self.halvings):
            near, far = (
                self.identity(*[mask if axis == name else 0 for name in AXES])
                for axis, mask in (self.orders[0][step], self.orders[1][step])
            )
            flip = near + core * (far - near)
            pieces = [piece ^ turned for piece in pieces for turned in (0, flip)]
        return pieces


def reduce_scatter(plan, own, other):
    for step in range(-1, len(plan.orders[0])):
        received = lax.ppermute(other, AXES, plan.permutation(step))
        if step + 1 == len(plan.orders[0]):
            break
        if step + 1 < plan.halvings:
            half = own.shape[0] // 2
            own, other = own[:half] + received[:half], own[half:] + received[half:]
        else:
            own = own + received
            other = own
    return own, received


def all_gather(plan, piece):
    parts = [piece]
    for step in reversed(range(plan.halvings)):
        whole = parts[0] if len(parts) == 1 else jnp.concatenate(parts)
        parts = [whole, lax.ppermute(whole, AXES, plan.permutation(step))]
    return parts + [lax.ppermute(part, AXES, plan.permutation(-1)) for part in parts]


def lane(shape):
    return lax.broadcasted_iota(jnp.int32, shape, len(shape) - 1)


def swap(value):
    return pltpu.roll(value, NG, value.ndim - 1)


def cut(value):
    high = value.astype(BF16)
    return high, (value - high.astype(F32)).astype(BF16)


def product(left, right):
    return lax.dot_general(left, right, (((1,), (0,)), ((), ())), preferred_element_type=F32)


def times_table(value, table):
    high, low = cut(value)
    leading = jnp.concatenate([table[0], table[0]])
    return product(jnp.concatenate([high, low], axis=1), leading) + product(high, table[1])


def table_times(table, value):
    high, low = cut(value)
    return product(table[0], high) + (product(table[0], low) + product(table[1], high))


def fold(near, far):
    low = lane(near.shape) < NG
    return jnp.where(low, near, swap(far)), jnp.where(low, swap(near), far)


def unfold(even, odd):
    low = lane(even.shape) < NG
    return jnp.where(low, even, swap(odd)), jnp.where(low, swap(even), odd)


def deal(plan, whole_ref, own_ref, other_ref):
    rows = ROWS // plan.pieces
    for side, out_ref in enumerate((own_ref, other_ref)):
        for index, piece in enumerate(plan.places(side)):
            out_ref[index] = whole_ref[pl.ds(pl.multiple_of(piece * rows, 8), rows), :]


def collect(plan, part_refs, store):
    rows = ROWS // plan.pieces
    for side in range(2):
        for index, piece in enumerate(plan.places(side)):
            part, at = divmod(index, plan.pieces // 4)
            store(pl.ds(pl.multiple_of(piece * rows, 8), rows), part_refs[2 * side + part][at])


def kappa_kernel(plans, scale, state_ref, *refs):
    out_refs, psi_ref, whole_refs, arrived = refs[:4], refs[4], refs[5:7], refs[7]
    waves, rows = psi_ref.shape[0], ROWS // CHUNKS
    copies = [
        [
            pltpu.make_async_copy(
                state_ref.at[wave, pl.ds(chunk * rows, rows), c, :],
                psi_ref.at[wave, c, pl.ds(chunk * rows, rows), :],
                arrived.at[chunk, wave, c],
            )
            for wave in range(waves)
            for c in range(4)
        ]
        for chunk in range(CHUNKS)
    ]
    for chunk in copies:
        for copy in chunk:
            copy.start()

    for chunk in range(CHUNKS):
        for copy in copies[chunk]:
            copy.wait()

        def body(plane, carry, chunk=chunk):
            where = pl.ds(pl.multiple_of(chunk * rows + plane * PLANE, 8), PLANE)
            real = imag = None
            for wave in range(waves):
                u_real, u_imag, v_real, v_imag = (psi_ref[wave, c, where, :] for c in range(4))
                add_real = u_real * v_real + u_imag * v_imag
                add_imag = u_imag * v_real - u_real * v_imag
                real = add_real if real is None else real + add_real
                imag = add_imag if imag is None else imag + add_imag
            whole_refs[0][where, :] = real * scale
            whole_refs[1][where, :] = imag * scale
            return carry

        lax.fori_loop(0, rows // PLANE, body, 0)
    for which, plan in enumerate(plans):
        deal(plan, whole_refs[which], out_refs[2 * which], out_refs[2 * which + 1])


def density_kernel(plan, scale, psi_ref, y_ref, z_ref, own_ref, other_ref, spectrum_ref):
    half = NX // 2

    def density(plane):
        where = pl.ds(pl.multiple_of(plane * PLANE, 8), PLANE)
        total = None
        for wave in range(psi_ref.shape[0]):
            real, imag = psi_ref[wave, 2, where, :], psi_ref[wave, 3, where, :]
            value = real * real + imag * imag
            total = value if total is None else total + value
        return total * scale

    def body(block, carry):
        for group in range(NX // 2 // GROUP):
            parts = []
            for j in range(GROUP):
                plane = group * GROUP + j
                parts += fold(density(plane), density(plane + half))
            value = times_table(jnp.concatenate(parts), z_ref)
            value = table_times(y_ref, value)
            for j in range(GROUP):
                spectrum_ref[pl.ds(group * GROUP + j, NG, stride=half), :] = value[j * NG : (j + 1) * NG]
        return carry

    body(0, 0)
    deal(plan, spectrum_ref, own_ref, other_ref)


def coulomb_kernel(plan, own_ref, received_ref, even_ref, odd_ref, xz_ref, y_ref, out_ref):
    half = NX // 2
    low_lanes = lane((half, LANES)) < NG
    sign = jnp.where(low_lanes, 1.0, -1.0)
    count = ROWS // plan.pieces // half
    first = plan.identity(lax.axis_index("grp"), lax.axis_index("wf")) * count

    def dot(matrix, value, axis):
        return lax.dot_general(
            matrix, value, (((axis,), (0,)), ((), ())),
            precision=lax.Precision.HIGHEST, preferred_element_type=F32,
        )

    for k in range(count):
        rows = pl.ds(k * half, half)
        value = own_ref[0, rows, :] + received_ref[0, rows, :]
        value = swap(value) + sign * value
        value = jnp.where(low_lanes, dot(even_ref[...], value, 1), dot(odd_ref[...], value, 1))
        squared = xz_ref[...] + y_ref[first + k]
        kernel = jnp.where(
            squared > 0.001,
            4.0 * math.pi * coulomb_coef / jnp.where(squared > 0.001, squared, 1.0),
            0.0,
        )
        value = value * (density_coef + kernel)
        value = jnp.where(low_lanes, dot(even_ref[...], value, 0), dot(odd_ref[...], value, 0))
        out_ref[0, rows, :] = swap(value) + sign * value


def mean_kernel(plan, *refs):
    part_refs, (outer_ref, y_ref, z_ref, out_ref, spectrum_ref) = refs[:4], refs[4:]
    half = NX // 2

    def store(where, value):
        spectrum_ref[where, :] = value

    collect(plan, part_refs, store)

    def body(block, carry):
        for group in range(NX // 2 // GROUP):
            value = jnp.concatenate(
                [spectrum_ref[pl.ds(group * GROUP + j, NG, stride=half), :] for j in range(GROUP)]
            )
            value = table_times(y_ref, value)
            value = times_table(value, z_ref)
            for j in range(GROUP):
                at = j * NG
                natural = unfold(value[at : at + PLANE], value[at + PLANE : at + NG])
                for x, part in zip((group * GROUP + j, group * GROUP + j + half), natural):
                    where = pl.ds(pl.multiple_of(x * PLANE, 8), PLANE)
                    out_ref[where, :] = part + outer_ref[where, :]
        return carry

    body(0, 0)


def propagate_kernel(plans, *refs):
    (psi_ref, mean_ref, coupling_ref, shift_ref), refs = refs[:4], refs[4:]
    parts, refs = (refs[:4], refs[4:8]), refs[8:]
    out_ref, potentials_ref, single_ref, real_ref, imag_ref, inner_ref, swapped_ref = refs[:7]
    (*buffers, left) = refs[7:]
    terms = [psi_ref.at[0]] + buffers

    for plan, part_refs, pair_ref in zip(plans, parts, (real_ref, imag_ref)):

        def store(where, value, pair_ref=pair_ref):
            pair_ref[where, :] = -2.0 * coupling_ref[where, :] * value

        collect(plan, part_refs, store)

    def prepare(plane, carry):
        where = pl.ds(pl.multiple_of(plane * PLANE, 8), PLANE)
        single_ref[where, :] = 2.0 * mean_ref[where, :] + 12.0 * kinetic_coef
        return carry

    lax.fori_loop(0, NX, prepare, 0)

    planes, width = potentials_ref.shape[1:]
    start = lax.axis_index("grp") * planes * PLANE + lax.axis_index("wf") * (width // LANES)
    for which, (ref, factor) in enumerate(((mean_ref, 1.0), (real_ref, 0.5), (imag_ref, 0.5))):
        for j in range(width // LANES):
            value = ref[pl.ds(start + j, planes, stride=PLANE), :]
            potentials_ref[which, :, j * LANES : (j + 1) * LANES] = factor * value

    low_lanes = lane((8, LANES)) < NG

    def in_lanes(source, first, slot):
        value = jnp.concatenate(
            [
                source[c, pl.ds(pl.multiple_of((first + p) * PLANE, 8), PLANE), :]
                for p in range(STEP)
                for c in range(4)
            ]
        )
        moved = product(jnp.concatenate(cut(value), axis=1), shift_ref[...])
        inner_ref[slot] = moved[:, :LANES]
        for k in range(4 * STEP):
            rows = moved[k * PLANE : (k + 1) * PLANE, LANES:]
            swapped_ref[slot, k, PAD : PAD + PLANE] = rows
            swapped_ref[slot, k, PAD - 1 : PAD] = rows[PLANE - 1 :]
            swapped_ref[slot, k, PAD + PLANE : PAD + PLANE + 1] = rows[:1]

    weights = [(0.5 * time_step) ** k / math.factorial(k) for k in range(5)]

    def finish(stage, plane, p, slot):
        source = terms[stage - 1]
        base = pl.multiple_of(plane * PLANE, 8)
        before = pl.multiple_of(((plane + NX - 1) & (NX - 1)) * PLANE, 8)
        after = pl.multiple_of(((plane + 1) & (NX - 1)) * PLANE, 8)
        for chunk in range(PLANE // 8):
            where = pl.ds(base + chunk * 8, 8)
            single, real, imag = single_ref[where, :], real_ref[where, :], imag_ref[where, :]
            state, total = [], []
            for c in range(4):
                k = p * 4 + c
                at = PAD + chunk * 8
                state.append(source[c, where, :])
                total.append(
                    (source[c, pl.ds(before + chunk * 8, 8), :] + source[c, pl.ds(after + chunk * 8, 8), :])
                    + (
                        inner_ref[slot, k * PLANE + chunk * 8 : k * PLANE + chunk * 8 + 8]
                        + jnp.where(
                            low_lanes,
                            swapped_ref[slot, k, at - 1 : at + 7],
                            swapped_ref[slot, k, at + 1 : at + 9],
                        )
                    )
                )
            values = (
                (single * state[1] - total[1]) + (real * state[3] + imag * state[2]),
                (total[0] - single * state[0]) + (imag * state[3] - real * state[2]),
                (total[3] - single * state[3]) + (real * state[1] - imag * state[0]),
                (single * state[2] - total[2]) - (real * state[0] + imag * state[1]),
            )
            for c in range(4):
                if stage == 4:
                    result = terms[1][c, where, :] + state[c] * weights[3]
                    terms[1][c, where, :] = result + values[c] * weights[4]
                else:
                    terms[stage][c, where, :] = values[c]
                if stage == 3:
                    result = terms[0][c, where, :] + terms[1][c, where, :] * weights[1]
                    terms[1][c, where, :] = result + state[c] * weights[2]

    block = SLOTS * STEP

    def leave(index, c):
        where = pl.ds(pl.multiple_of(index * (block * PLANE), 8), block * PLANE)
        return pltpu.make_async_copy(terms[1].at[c, where, :], out_ref.at[where, c, :], left.at[index, c])

    for stage in range(1, 5):
        for part in range(AHEAD):
            in_lanes(terms[stage - 1], part * STEP, part)

        def body(index, carry, stage=stage):
            for part in range(SLOTS):
                for p in range(STEP):
                    finish(stage, index * block + part * STEP + p, p, part)
                ahead = (index * block + (part + AHEAD) * STEP) & (NX - 1)
                in_lanes(terms[stage - 1], ahead, (part + AHEAD) % SLOTS)
            if stage == 4:
                for c in range(4):
                    leave(index, c).start()
            return carry

        lax.fori_loop(0, NX // block, body, 0)
    for index in range(NX // block):
        for c in range(4):
            leave(index, c).wait()


VMEM = pl.BlockSpec(memory_space=pltpu.VMEM)
ANY = pl.BlockSpec(memory_space=pl.ANY)
HBM = pl.BlockSpec(memory_space=pltpu.HBM)
SMEM = pl.BlockSpec(memory_space=pltpu.SMEM)


def call(kernel, name, out_shapes, operands, scratch=(), in_specs=None, out_specs=None, limit=16, flags=None):
    moved = sum(math.prod(o.shape) * 4 for o in (*out_shapes, *operands))
    return pl.pallas_call(
        kernel,
        name=name,
        out_shape=[jax.ShapeDtypeStruct(o.shape, o.dtype) for o in out_shapes],
        in_specs=in_specs or [VMEM] * len(operands),
        out_specs=out_specs or [VMEM] * len(out_shapes),
        scratch_shapes=[pltpu.VMEM(s, F32) if isinstance(s, tuple) else s for s in scratch],
        compiler_params=pltpu.CompilerParams(vmem_limit_bytes=limit * 1024 * 1024, flags=flags),
        cost_estimate=pl.CostEstimate(flops=0, bytes_accessed=moved, transcendentals=0),
    )(*operands)


def like(*shape):
    return jax.ShapeDtypeStruct(shape, F32)


def local(quasi, outer_field, coupling):
    sizes = {name: lax.axis_size(name) for name in AXES}
    devices = sizes["grp"] * sizes["wf"]
    waves = quasi.shape[0]
    scale = 1.0 / (waves * devices)
    bits = [("grp", 1 << k) for k in range(1, sizes["grp"].bit_length() - 1)]
    bits += [("wf", 1 << k) for k in range(sizes["wf"].bit_length() - 1)]
    first, second, third, rest = bits[0], bits[1], bits[2], bits[3:]
    straight = [first, second, third] + rest
    crossed = [second, first, third] + rest
    real_plan = Plan(sizes, (straight, crossed), devices)
    imag_plan = Plan(sizes, (crossed, straight), devices)
    mean_plan = Plan(sizes, ([third, first, second] + rest, [third, second, first] + rest), min(devices, NG))
    tables = {name: jnp.asarray(table) for name, table in transform_tables().items()}

    def halves(plan):
        return [like(plan.pieces // 2, ROWS // plan.pieces, LANES)] * 2

    state = pltpu.with_memory_space_constraint(quasi.reshape(waves, 4, ROWS, LANES).transpose(0, 2, 1, 3), pltpu.HBM)
    outer_field = outer_field.reshape(ROWS, LANES)
    coupling = coupling.reshape(ROWS, LANES)

    real_own, real_other, imag_own, imag_other, psi = call(
        functools.partial(kappa_kernel, (real_plan, imag_plan), scale),
        "kappa", halves(real_plan) + halves(imag_plan) + [like(waves, 4, ROWS, LANES)], [state],
        [(ROWS, LANES)] * 2 + [pltpu.SemaphoreType.DMA((CHUNKS, waves, 4))], in_specs=[HBM],
    )
    mean_own, mean_other = call(
        functools.partial(density_kernel, mean_plan, scale),
        "density", halves(mean_plan), [psi, tables["forward_y"], tables["forward_z"]], [(ROWS, LANES)],
    )
    real = reduce_scatter(real_plan, real_own, real_other)
    imag = reduce_scatter(imag_plan, imag_own, imag_other)
    mean = reduce_scatter(mean_plan, mean_own, mean_other)
    (spectrum,) = call(
        functools.partial(coulomb_kernel, mean_plan),
        "coulomb", [like(*mean[0].shape)],
        [*mean, tables["even"], tables["odd"], tables["symbol_xz"], tables["symbol_y"]],
        in_specs=[VMEM] * 5 + [SMEM],
    )
    mean_parts = all_gather(mean_plan, spectrum)
    real_parts = all_gather(real_plan, real[0] + real[1])
    imag_parts = all_gather(imag_plan, imag[0] + imag[1])
    (mean_field,) = call(
        functools.partial(mean_kernel, mean_plan),
        "mean", [like(ROWS, LANES)],
        [*mean_parts, outer_field, tables["inverse_y"], tables["inverse_z"]], [(ROWS, LANES)],
    )

    evolved = []
    for wave in range(waves):
        evolved_rows, potentials = call(
            functools.partial(propagate_kernel, (real_plan, imag_plan)),
            "propagate",
            [like(ROWS, 4, LANES), like(3, NX // sizes["grp"], NG * NG // sizes["wf"])],
            [psi[wave : wave + 1], mean_field, coupling, tables["shift"], *real_parts, *imag_parts],
            [(ROWS, LANES)] * 3
            + [(SLOTS, 4 * STEP * PLANE, LANES), (SLOTS, 4 * STEP, PADDED, LANES)]
            + [(4, ROWS, LANES)] * 3
            + [pltpu.SemaphoreType.DMA((NX // (SLOTS * STEP), 4))],
            out_specs=[ANY, VMEM],
            limit=32,
            flags=FLAGS,
        )
        evolved.append(evolved_rows)
    evolved = jnp.stack(evolved) if waves > 1 else evolved[0][None]
    evolved = evolved.transpose(0, 2, 1, 3).reshape(quasi.shape)
    return (evolved, potentials)


def solution(mesh):
    placed = (P(AXES, None, None), P(), P())
    return jax.shard_map(
        local,
        mesh=mesh,
        in_specs=placed,
        out_specs=(P(AXES, None, None), P(None, "grp", "wf")),
        check_vma=False,
    )
```
